256 devices in a mesh: sweep: 8 (over y, core), layer: 32 (over z, x).
Axes of the slice: x: 4, y: 4, z: 8, core: 2. Of those that a mesh axis runs over, the one named last changes fastest.
Arguments:
- face_rhs: float32 [8, 16, 128, 384], P('sweep', None, 'layer'), may hold values from -6 to 6
- res_rows: float32 [131072, 384], P(('sweep', 'layer')), may hold values from -4 to 4
- row_owner: int32 [131072, 1], P(('sweep', 'layer')), may hold values from 0 to 31; in each aligned block of 512 rows (0 to 511, 512 to 1023, ...) at most 32 rows name the same one
- row_slot: int32 [131072], P(('sweep', 'layer')), may hold values from 0 to 63
- inv_blocks: bfloat16 [8, 128, 384, 384], P('sweep', 'layer'), may hold values from -0.3125 to 0.3125
- couple_in: bfloat16 [8, 1536, 49152], P('sweep', None, 'layer'), may hold values from -0.15625 to 0.15625
- couple_out: bfloat16 [8, 49152, 1536], P('sweep', 'layer'), may hold values from -0.02734375 to 0.02734375
Outputs:
- solved: float32 [8, 16, 128, 384], P('sweep', None, 'layer')
The draws below stay inside these ranges and needn't reach their ends.
Inputs may be any that keep to these rules, and one draw needn't show every extreme that they name: `row_owner`: among the 512 rows of one device no owner is named by more than 32 rows, a bound that some block reaches.
All inputs are finite; a program needn't handle non-finite values.
Results may differ from the reference program's by a relative error of at most 0.02.
Values may be sent and summed in bfloat16 or wider, within the bound.
No kernel may reach another device: no remote copies, remote signals or barrier semaphores. Data moves between devices by JAX's collectives and lax.ppermute only.
A program may use at most 64 MiB of HBM per device.

```python
import math
import jax
import jax.numpy as jnp
import numpy as np

W = 384
P_SIZE = 1536
R = 16
FACE_DEV = 4
ROW_DEV = 512
LAYERS = 8
FACES = 128
CAP = 32
ROWS = 131072
N_LAYER = 32


def plant(entries, key, least, top_value):
    spot = [jax.random.randint(jax.random.fold_in(key, axis), (), 0, length) for axis, length in enumerate(entries.shape)]
    widest = entries.shape.index(max(entries.shape))
    next_to = spot[:widest] + [(spot[widest] + 1) % entries.shape[widest]] + spot[widest + 1:]
    return entries.at[tuple(spot)].set(least).at[tuple(next_to)].set(top_value)


def shard_levels(stream_key, extent, split, least, high):
    loudness, own = 1.0, jax.random.fold_in(stream_key, 6)
    for position, blocks in split:
        steps = jnp.exp(jax.random.uniform(jax.random.fold_in(own, position), (blocks,), jnp.float32, least / len(split), high / len(split)))
        loudness = loudness * jnp.repeat(steps, extent[position] // blocks).reshape([-1 if axis == position else 1 for axis in range(len(extent))])
    return loudness


def deal_out(stream_key, own, number, rows, amount, top, reach, slope):
    order = jax.random.permutation(stream_key, amount)
    packed, usual = portions_of(amount, rows * top, reach, slope, True), portions_of(amount, rows * top, reach, slope, False)
    places = jnp.arange(amount)

    def named(lengths, rotation):
        used = int((lengths > 0).sum())
        fixed = max(1, used // 4)
        moved = fixed + (places - fixed + rotation * (used - fixed)) % max(1, amount - fixed)
        return jnp.zeros((amount,), jnp.int32).at[order[jnp.where(places < fixed, places, moved)]].set(jnp.asarray(lengths, jnp.int32))

    lengths = jnp.where(number % 4 == 0, named(packed, number // 4), named(usual, number - number // 4 - 1))
    mixed = jax.random.permutation(jax.random.fold_in(own, 3), amount)
    source_of, taker = mixed[0:amount // 2 * 2:2], mixed[1:amount // 2 * 2:2]
    slack = jnp.minimum(lengths[source_of] - 1, reach - lengths[taker]) // 2
    slack = jnp.where((source_of == order[0]) | (taker == order[0]) | (lengths[taker] == 0), 0, jnp.maximum(slack, 0))
    moved = jax.random.randint(jax.random.fold_in(own, 4), (amount // 2,), 0, 1 << 20) % (slack + 1)
    lengths = lengths.at[source_of].add(-moved).at[taker].add(moved)
    labels = jnp.searchsorted(jnp.cumsum(lengths), jnp.arange(rows * top), side="right").astype(jnp.int32)
    table = labels.reshape(top, rows).T
    table = table[jax.random.permutation(jax.random.fold_in(own, 1), rows)]
    rotation = jax.random.randint(jax.random.fold_in(own, 2), (rows, 1), 0, top)
    return jnp.take_along_axis(table, (jnp.arange(top)[None, :] + rotation) % top, axis=1)


def portions_of(number_of, total, bound, skew, full):
    loads = [(1 << 20) // math.isqrt(rank ** skew) + 1 for rank in range(1, number_of + 1)]
    largest = bound if full else min(bound, max(-(-total // number_of), total * loads[0] // sum(loads)))
    least = 1 if total - largest >= number_of - 1 else 0
    holding, surplus = [largest] + [least] * (number_of - 1), total - largest - least * (number_of - 1)
    while surplus > 0:
        candidates = [i for i in range(1, number_of) if holding[i] < largest] or [i for i in range(1, number_of) if holding[i] < bound]
        pool, budget = sum([loads[i] for i in candidates]), surplus
        for i in candidates:
            extra = min(bound - holding[i], max(1, budget * loads[i] // pool), surplus)
            holding[i] = holding[i] + extra
            surplus = surplus - extra
    return np.array(holding)


def scatter_about(rng, dims, width, most, shards=(), kind=jnp.bfloat16):
    array = jax.random.normal(rng, dims, jnp.float32) * width
    if len(shards) > 0:
        array = shard_levels(rng, dims, shards, -0.22, 0.18) * array
    return jnp.clip(array, min=-most, max=most).astype(kind)


def setup_inputs(seed: int = 0) -> dict:
    splits = jax.random.split(jax.random.key(seed), 8)
    face_rhs = scatter_about(splits[0], (LAYERS, R, FACES, W), 1.0, 6.0, ((0, 8), (2, 32)), jnp.float32)
    res_rows = scatter_about(splits[1], (ROWS, W), 0.5, 4.0, ((0, 256),), jnp.float32)
    row_owner_keys = jax.random.split(jax.random.fold_in(splits[2], 1), ROWS // ROW_DEV)
    row_owner_turns = jax.random.permutation(jax.random.fold_in(splits[2], 3), ROWS // ROW_DEV)
    row_owner = jax.vmap(lambda own, number: deal_out(jax.random.fold_in(splits[2], 2), own, number, ROW_DEV, N_LAYER, 1, CAP, 2))(row_owner_keys, row_owner_turns).reshape((ROWS, 1))
    row_slot = plant(jax.random.randint(splits[3], (ROWS,), 0, FACE_DEV * R), jax.random.fold_in(splits[3], 1), 0, (FACE_DEV * R) - 1).astype(jnp.int32)
    inv_blocks = scatter_about(splits[4], (LAYERS, FACES, W, W), W ** -0.5, 0.3125, ((0, 8), (1, 32)))
    couple_in = scatter_about(splits[5], (LAYERS, P_SIZE, FACES * W), P_SIZE ** -0.5, 0.15625, ((0, 8), (2, 32)))
    couple_out = scatter_about(splits[6], (LAYERS, FACES * W, P_SIZE), (FACES * W) ** -0.5, 0.02734375, ((0, 8), (1, 32)))
    return dict(face_rhs=face_rhs, res_rows=res_rows, row_owner=row_owner, row_slot=row_slot, inv_blocks=inv_blocks, couple_in=couple_in, couple_out=couple_out)


def reference(face_rhs, res_rows, row_owner, row_slot, inv_blocks, couple_in, couple_out):
    row_index = jnp.arange(ROWS, dtype=jnp.int32)
    layer_of_row = row_index // (ROW_DEV * N_LAYER)
    rhs_of_row = row_slot // FACE_DEV
    face_of_row = row_owner[:, 0] * FACE_DEV + row_slot % FACE_DEV
    target = ((layer_of_row * R + rhs_of_row) * FACES + face_of_row).astype(jnp.int32)
    added_rows = jax.ops.segment_sum(res_rows, target, num_segments=LAYERS * R * FACES)
    assembled = face_rhs + added_rows.reshape(LAYERS, R, FACES, W)
    panel_in = jnp.zeros((R, P_SIZE), jnp.float32)
    results = []
    for layer_step in range(LAYERS):
        coupled = jnp.dot(panel_in.astype(jnp.bfloat16), couple_in[layer_step], preferred_element_type=jnp.float32)
        local_part = (assembled[layer_step] - coupled.reshape(R, FACES, W)).astype(jnp.bfloat16)
        solved = jnp.einsum("rfw,fwv->rfv", local_part.astype(jnp.float32), inv_blocks[layer_step].astype(jnp.float32))
        results.append(solved)
        flattened = solved.astype(jnp.bfloat16).reshape(R, FACES * W)
        panel_in = jnp.dot(flattened, couple_out[layer_step], preferred_element_type=jnp.float32)
    return jnp.stack(results)
```

```python
import jax
import jax.numpy as jnp
from jax import lax
from jax.experimental import pallas as pl
from jax.experimental.pallas import tpu as pltpu
from jax.sharding import Mesh
from jax.sharding import PartitionSpec as P

BF = jnp.bfloat16
F32 = jnp.float32
LANES = 128


def pack_kernel(owner_count, owner_ref, slot_ref, rows_ref, out_ref):
    row_total, width = rows_ref.shape
    capacity = row_total // owner_count * 2
    owner = owner_ref[...]
    match = (lax.broadcasted_iota(jnp.int32, (owner_count, row_total), 0) == owner).astype(F32)
    earlier_mask = (
        lax.broadcasted_iota(jnp.int32, (row_total, row_total), 0)
        < lax.broadcasted_iota(jnp.int32, (row_total, row_total), 1)
    )
    earlier = jnp.dot(
        match.astype(BF), earlier_mask.astype(F32).astype(BF), preferred_element_type=F32
    )
    position = jnp.sum(earlier * match, axis=0, keepdims=True).astype(jnp.int32)
    target = owner * capacity + position
    slots = (slot_ref[...] + 1).astype(F32)
    rows = rows_ref[...].astype(BF)
    block = 256
    for start in range(0, owner_count * capacity, block):
        place = lax.broadcasted_iota(jnp.int32, (block, row_total), 0) + start
        chosen = place == target
        picked = jnp.where(chosen, 1.0, 0.0).astype(BF)
        out_ref[pl.ds(start, block), pl.ds(0, width)] = jnp.dot(
            picked, rows, preferred_element_type=F32
        ).astype(BF)
        slot = jnp.sum(jnp.where(chosen, slots, 0.0), axis=1, keepdims=True)
        out_ref[pl.ds(start, block), pl.ds(width, LANES)] = jnp.broadcast_to(
            slot, (block, LANES)
        ).astype(BF)


def unpack_kernel(face_dev, got_ref, face_ref, out_ref):
    rhs_count = out_ref.shape[0]
    width = out_ref.shape[1] // face_dev
    slot = got_ref[:, pl.ds(width, LANES)].astype(F32)
    lane = lax.broadcasted_iota(jnp.int32, slot.shape, 1)
    wanted = (lane % rhs_count) * face_dev + lane // rhs_count + 1
    wanted = jnp.where(lane < rhs_count * face_dev, wanted, -1).astype(F32)
    picked = jnp.where(slot == wanted, 1.0, 0.0).astype(BF)
    summed = lax.dot_general(
        picked,
        got_ref[:, pl.ds(0, width)],
        (((0,), (0,)), ((), ())),
        preferred_element_type=F32,
    )
    for face in range(face_dev):
        out_ref[:, pl.ds(face * width, width)] = (
            face_ref[:, face, :] + summed[face * rhs_count : (face + 1) * rhs_count, :]
        )


def on_device(shape, face_rhs, res_rows, row_owner, row_slot, inv_blocks, couple_in, couple_out):
    sweep_count, z_count, x_count = shape
    group_size = z_count * x_count
    rhs_count, face_dev, width = face_rhs.shape[1:]
    row_total = res_rows.shape[0]
    capacity = 2 * row_total // group_size
    coupling_in, coupling_out, inverse = couple_in[0], couple_out[0], inv_blocks[0]

    with jax.named_scope("pack"):
        packed = pl.pallas_call(
            lambda *refs: pack_kernel(group_size, *refs),
            out_shape=jax.ShapeDtypeStruct((group_size * capacity, width + LANES), BF),
            name="pack",
        )(row_owner.reshape(1, row_total), row_slot.reshape(1, row_total), res_rows)
    with jax.named_scope("route"):
        got = lax.all_to_all(
            packed.reshape(group_size, capacity, width + LANES),
            ("z", "x"),
            split_axis=0,
            concat_axis=0,
            tiled=True,
        ).reshape(group_size * capacity, width + LANES)
    with jax.named_scope("fold"):
        outward = jnp.einsum(
            "fwv,fvp->fwp",
            inverse,
            coupling_out.reshape(face_dev, width, -1),
            preferred_element_type=F32,
        )
        outward = outward.astype(BF).reshape(face_dev * width, -1)
        through = jnp.dot(coupling_in, outward, preferred_element_type=F32).astype(BF)
    with jax.named_scope("unpack"):
        assembled = pl.pallas_call(
            lambda *refs: unpack_kernel(face_dev, *refs),
            out_shape=jax.ShapeDtypeStruct((rhs_count, face_dev * width), F32),
            name="unpack",
        )(got, face_rhs[0])
    with jax.named_scope("source"):
        high = assembled.astype(BF)
        low = (assembled - high.astype(F32)).astype(BF)
        both = jnp.dot(
            jnp.concatenate([high, low], axis=0), outward, preferred_element_type=F32
        )
        source = both[:rhs_count] + both[rhs_count:]

    def number(s, z, x):
        return (s * z_count + z) * x_count + x

    def exchange(value, layer, mask_x, mask_z, shift=0):
        pairs = [
            (number(layer, z, x), number(layer + shift, z ^ mask_z, x ^ mask_x))
            for z in range(z_count)
            for x in range(x_count)
        ]
        return lax.ppermute(value, ("sweep", "z", "x"), pairs)

    def total(values):
        result = values[0].astype(F32)
        for value in values[1:]:
            result = result + value.astype(F32)
        return result

    panel = None
    arrived = []
    for layer in range(sweep_count - 1):
        with jax.named_scope("stage%d" % layer):
            part = source
            if panel is not None:
                part = source - jnp.dot(panel, through, preferred_element_type=F32)
            part = part.astype(BF)
            part = total([part] + [exchange(part, layer, m, 0) for m in range(1, x_count)])
            part = part.astype(BF)
            part = total([part] + [exchange(part, layer, 0, m) for m in range(1, z_count // 2)])
            part = part.astype(BF)
            panel = total(
                [exchange(part, layer, 0, m, 1) for m in (0, z_count - 1)]
            ).astype(BF)
            arrived.append(panel)
    with jax.named_scope("solve"):
        panel = total(arrived).astype(BF)
        coupled = jnp.dot(panel, coupling_in, preferred_element_type=F32)
        local = (assembled - coupled).astype(BF).reshape(rhs_count, face_dev, width)
        solved = jnp.einsum("rfw,fwv->rfv", local, inverse, preferred_element_type=F32)
    return solved[None]


def solution(mesh):
    shape = (mesh.shape["sweep"], 8, mesh.shape["layer"] // 8)
    fine = Mesh(mesh.devices.reshape(shape), ("sweep", "z", "x"))
    layer = ("z", "x")
    everywhere = ("sweep", "z", "x")
    return jax.shard_map(
        lambda *args: on_device(shape, *args),
        mesh=fine,
        in_specs=(
            P("sweep", None, layer, None),
            P(everywhere, None),
            P(everywhere, None),
            P(everywhere),
            P("sweep", layer, None, None),
            P("sweep", None, layer),
            P("sweep", layer, None),
        ),
        out_specs=P("sweep", None, layer, None),
        check_vma=False,
    )
```

```python
import jax
import jax.numpy as jnp
from jax import lax
from jax.experimental import pallas as pl
from jax.experimental.pallas import tpu as pltpu
from jax.sharding import Mesh
from jax.sharding import PartitionSpec as P

BF = jnp.bfloat16
F32 = jnp.float32
LANES = 128
SWITCH = 7


def pack_kernel(owner_count, owner_ref, slot_ref, rows_ref, out_ref):
    row_total, width = rows_ref.shape
    capacity = row_total // owner_count * 2
    owner = owner_ref[...]
    match = (lax.broadcasted_iota(jnp.int32, (owner_count, row_total), 0) == owner).astype(F32)
    earlier_mask = (
        lax.broadcasted_iota(jnp.int32, (row_total, row_total), 0)
        < lax.broadcasted_iota(jnp.int32, (row_total, row_total), 1)
    )
    earlier = jnp.dot(
        match.astype(BF), earlier_mask.astype(F32).astype(BF), preferred_element_type=F32
    )
    position = jnp.sum(earlier * match, axis=0, keepdims=True).astype(jnp.int32)
    target = owner * capacity + position
    slots = (slot_ref[...] + 1).astype(F32)
    rows = rows_ref[...].astype(BF)
    block = 256
    for start in range(0, owner_count * capacity, block):
        place = lax.broadcasted_iota(jnp.int32, (block, row_total), 0) + start
        chosen = place == target
        picked = jnp.where(chosen, 1.0, 0.0).astype(BF)
        out_ref[pl.ds(start, block), pl.ds(0, width)] = jnp.dot(
            picked, rows, preferred_element_type=F32
        ).astype(BF)
        slot = jnp.sum(jnp.where(chosen, slots, 0.0), axis=1, keepdims=True)
        out_ref[pl.ds(start, block), pl.ds(width, LANES)] = jnp.broadcast_to(
            slot, (block, LANES)
        ).astype(BF)


def unpack_kernel(face_dev, got_ref, face_ref, out_ref):
    rhs_count = out_ref.shape[0]
    width = out_ref.shape[1] // face_dev
    slot = got_ref[:, pl.ds(width, LANES)].astype(F32)
    lane = lax.broadcasted_iota(jnp.int32, slot.shape, 1)
    wanted = (lane % rhs_count) * face_dev + lane // rhs_count + 1
    wanted = jnp.where(lane < rhs_count * face_dev, wanted, -1).astype(F32)
    picked = jnp.where(slot == wanted, 1.0, 0.0).astype(BF)
    summed = lax.dot_general(
        picked,
        got_ref[:, pl.ds(0, width)],
        (((0,), (0,)), ((), ())),
        preferred_element_type=F32,
    )
    for face in range(face_dev):
        out_ref[:, pl.ds(face * width, width)] = (
            face_ref[:, face, :] + summed[face * rhs_count : (face + 1) * rhs_count, :]
        )


def on_device(shape, face_rhs, res_rows, row_owner, row_slot, inv_blocks, couple_in, couple_out):
    sweep_count, z_count, x_count = shape
    group_size = z_count * x_count
    rhs_count, face_dev, width = face_rhs.shape[1:]
    row_total = res_rows.shape[0]
    capacity = 2 * row_total // group_size
    coupling_in, coupling_out, inverse = couple_in[0], couple_out[0], inv_blocks[0]

    with jax.named_scope("pack"):
        packed = pl.pallas_call(
            lambda *refs: pack_kernel(group_size, *refs),
            out_shape=jax.ShapeDtypeStruct((group_size * capacity, width + LANES), BF),
            name="pack",
        )(row_owner.reshape(1, row_total), row_slot.reshape(1, row_total), res_rows)
    with jax.named_scope("route"):
        got = lax.all_to_all(
            packed.reshape(group_size, capacity, width + LANES),
            ("z", "x"),
            split_axis=0,
            concat_axis=0,
            tiled=True,
        ).reshape(group_size * capacity, width + LANES)
    with jax.named_scope("fold"):
        outward = jnp.einsum(
            "fwv,fvp->fwp",
            inverse,
            coupling_out.reshape(face_dev, width, -1),
            preferred_element_type=F32,
        )
        outward = outward.astype(BF).reshape(face_dev * width, -1)
        through = jnp.dot(coupling_in, outward, preferred_element_type=F32).astype(BF)
    with jax.named_scope("unpack"):
        assembled = pl.pallas_call(
            lambda *refs: unpack_kernel(face_dev, *refs),
            out_shape=jax.ShapeDtypeStruct((rhs_count, face_dev * width), F32),
            name="unpack",
        )(got, face_rhs[0])
    with jax.named_scope("source"):
        high = assembled.astype(BF)
        low = (assembled - high.astype(F32)).astype(BF)
        both = jnp.dot(
            jnp.concatenate([high, low], axis=0), outward, preferred_element_type=F32
        )
        source = both[:rhs_count] + both[rhs_count:]

    def number(s, z, x):
        return (s * z_count + z) * x_count + x

    def exchange(value, mask_x, mask_z, shift=0, first=0, step=1):
        pairs = [
            (number(s, z, x), number(s + shift, z ^ mask_z, x ^ mask_x))
            for s in range(first, sweep_count - shift, step)
            for z in range(z_count)
            for x in range(x_count)
        ]
        return lax.ppermute(value, ("sweep", "z", "x"), pairs)

    def total(values):
        result = values[0].astype(F32)
        for value in values[1:]:
            result = result + value.astype(F32)
        return result

    far = z_count - 1
    own_layer = lax.axis_index("sweep")
    if SWITCH < sweep_count - 1:
        with jax.named_scope("whole"):
            whole = lax.psum(through, ("z", "x"))
    panel = None
    for layer in range(sweep_count - 1):
        with jax.named_scope("stage%d" % layer):
            if layer < SWITCH:
                part = source
                if panel is not None:
                    part = source - jnp.dot(panel, through, preferred_element_type=F32)
                part = part.astype(BF)
                part = total([part] + [exchange(part, m, 0) for m in range(1, x_count)])
                part = part.astype(BF)
                part = total([part] + [exchange(part, 0, m) for m in range(1, z_count // 2)])
                part = part.astype(BF)
                panel = total([exchange(part, 0, m, 1) for m in (0, far)]).astype(BF)
                if layer == 0:
                    kept = part
            else:
                if layer == SWITCH:
                    whole_source = total([kept, exchange(kept, 0, far)])
                following = whole_source - jnp.dot(panel, whole, preferred_element_type=F32)
                sent = exchange(following.astype(BF), 0, 0, 1, layer % 2, 2)
                panel = jnp.where(own_layer == layer + 1, sent, panel)
    with jax.named_scope("solve"):
        coupled = jnp.dot(panel, coupling_in, preferred_element_type=F32)
        local = (assembled - coupled).astype(BF).reshape(rhs_count, face_dev, width)
        solved = jnp.einsum("rfw,fwv->rfv", local, inverse, preferred_element_type=F32)
    return solved[None]


def solution(mesh):
    shape = (mesh.shape["sweep"], 8, mesh.shape["layer"] // 8)
    fine = Mesh(mesh.devices.reshape(shape), ("sweep", "z", "x"))
    layer = ("z", "x")
    everywhere = ("sweep", "z", "x")
    return jax.shard_map(
        lambda *args: on_device(shape, *args),
        mesh=fine,
        in_specs=(
            P("sweep", None, layer, None),
            P(everywhere, None),
            P(everywhere, None),
            P(everywhere),
            P("sweep", layer, None, None),
            P("sweep", None, layer),
            P("sweep", layer, None),
        ),
        out_specs=P("sweep", None, layer, None),
        check_vma=False,
    )
```

```python
import jax
import jax.numpy as jnp
from jax import lax
from jax.experimental import pallas as pl
from jax.experimental.pallas import tpu as pltpu
from jax.sharding import Mesh
from jax.sharding import PartitionSpec as P

BF = jnp.bfloat16
F32 = jnp.float32
LANES = 128


def pack_kernel(owner_count, owner_ref, slot_ref, rows_ref, out_ref):
    row_total, width = rows_ref.shape
    capacity = row_total // owner_count * 2
    owner = owner_ref[...]
    match = (lax.broadcasted_iota(jnp.int32, (owner_count, row_total), 0) == owner).astype(F32)
    earlier_mask = (
        lax.broadcasted_iota(jnp.int32, (row_total, row_total), 0)
        < lax.broadcasted_iota(jnp.int32, (row_total, row_total), 1)
    )
    earlier = jnp.dot(
        match.astype(BF), earlier_mask.astype(F32).astype(BF), preferred_element_type=F32
    )
    position = jnp.sum(earlier * match, axis=0, keepdims=True).astype(jnp.int32)
    target = owner * capacity + position
    slots = (slot_ref[...] + 1).astype(F32)
    rows = rows_ref[...].astype(BF)
    block = 256
    for start in range(0, owner_count * capacity, block):
        place = lax.broadcasted_iota(jnp.int32, (block, row_total), 0) + start
        chosen = place == target
        picked = jnp.where(chosen, 1.0, 0.0).astype(BF)
        out_ref[pl.ds(start, block), pl.ds(0, width)] = jnp.dot(
            picked, rows, preferred_element_type=F32
        ).astype(BF)
        slot = jnp.sum(jnp.where(chosen, slots, 0.0), axis=1, keepdims=True)
        out_ref[pl.ds(start, block), pl.ds(width, LANES)] = jnp.broadcast_to(
            slot, (block, LANES)
        ).astype(BF)


def unpack_kernel(face_dev, got_ref, face_ref, out_ref):
    rhs_count = out_ref.shape[0]
    width = out_ref.shape[1] // face_dev
    slot = got_ref[:, pl.ds(width, LANES)].astype(F32)
    lane = lax.broadcasted_iota(jnp.int32, slot.shape, 1)
    wanted = (lane % rhs_count) * face_dev + lane // rhs_count + 1
    wanted = jnp.where(lane < rhs_count * face_dev, wanted, -1).astype(F32)
    picked = jnp.where(slot == wanted, 1.0, 0.0).astype(BF)
    summed = lax.dot_general(
        picked,
        got_ref[:, pl.ds(0, width)],
        (((0,), (0,)), ((), ())),
        preferred_element_type=F32,
    )
    for face in range(face_dev):
        out_ref[:, pl.ds(face * width, width)] = (
            face_ref[:, face, :] + summed[face * rhs_count : (face + 1) * rhs_count, :]
        )


def on_device(shape, face_rhs, res_rows, row_owner, row_slot, inv_blocks, couple_in, couple_out):
    sweep_count, z_count, x_count = shape
    group_size = z_count * x_count
    rhs_count, face_dev, width = face_rhs.shape[1:]
    row_total = res_rows.shape[0]
    capacity = 2 * row_total // group_size
    coupling_in, coupling_out, inverse = couple_in[0], couple_out[0], inv_blocks[0]

    with jax.named_scope("pack"):
        packed = pl.pallas_call(
            lambda *refs: pack_kernel(group_size, *refs),
            out_shape=jax.ShapeDtypeStruct((group_size * capacity, width + LANES), BF),
            name="pack",
        )(row_owner.reshape(1, row_total), row_slot.reshape(1, row_total), res_rows)
    with jax.named_scope("route"):
        got = lax.all_to_all(
            packed.reshape(group_size, capacity, width + LANES),
            ("z", "x"),
            split_axis=0,
            concat_axis=0,
            tiled=True,
        ).reshape(group_size * capacity, width + LANES)
    def number(s, z, x):
        return (s * z_count + z) * x_count + x

    def exchange(value, mask_x, mask_z, shift=0, first=0, step=1):
        pairs = [
            (number(s, z, x), number(s + shift, z ^ mask_z, x ^ mask_x))
            for s in range(first, sweep_count - shift, step)
            for z in range(z_count)
            for x in range(x_count)
        ]
        return lax.ppermute(value, ("sweep", "z", "x"), pairs)

    def total(values):
        result = values[0].astype(F32)
        for value in values[1:]:
            result = result + value.astype(F32)
        return result

    far = z_count - 1
    here_x, here_z = lax.axis_index("x"), lax.axis_index("z")
    odd = lax.axis_index("sweep") % 2 == 1
    panel_size = coupling_in.shape[0]
    slab = panel_size // x_count

    with jax.named_scope("fold"):
        outward = jnp.einsum(
            "fwv,fvp->fwp",
            inverse,
            coupling_out.reshape(face_dev, width, -1),
            preferred_element_type=F32,
        )
        outward = outward.astype(BF).reshape(face_dev * width, -1)

        def by_rows(masks):
            return [
                jnp.dot(
                    lax.dynamic_slice_in_dim(coupling_in, (here_x ^ m) * slab, slab, 0),
                    outward,
                    preferred_element_type=F32,
                ).astype(BF)
                for m in masks
            ]

        def by_columns(masks):
            return [
                lax.dot_general(
                    lax.dynamic_slice_in_dim(outward, (here_x ^ m) * slab, slab, 1),
                    coupling_in,
                    (((0,), (1,)), ((), ())),
                    preferred_element_type=F32,
                ).astype(BF)
                for m in masks
            ]

        def folded(*masks):
            return lax.cond(odd, lambda: by_rows(masks), lambda: by_columns(masks))

        (piece2,) = folded(2)
        piece1, piece3, piece0 = folded(1, 3, 0)
    with jax.named_scope("sum_x"):
        half = slab // 2
        upper = exchange(piece2[:half], 1, 0)
        lower = exchange(piece2[half:], 3, 0)
        to3 = jnp.concatenate([total([piece3[:half], upper]).astype(BF), piece3[half:]], axis=0)
        to1 = jnp.concatenate([piece1[:half], total([piece1[half:], lower]).astype(BF)], axis=0)
        summed_x = total([piece0, exchange(to3, 3, 0), exchange(to1, 1, 0)]).astype(BF)
    with jax.named_scope("sum_z"):
        four = z_count // 2
        spot = (here_z % four) ^ jnp.where(here_z >= four, four - 1, 0)
        quarter = slab // four
        quarters = [
            lax.dynamic_slice_in_dim(summed_x, (spot ^ m) * quarter, quarter, 0)
            for m in range(four)
        ]
        own = total([quarters[0]] + [exchange(quarters[m], 0, m) for m in range(1, four)])
        own = own.astype(BF)
        own = total([own, exchange(own, 0, far)]).astype(BF)
        through = jnp.zeros((slab, panel_size), BF)
        for m in range(four):
            part = own if m == 0 else exchange(own, 0, m)
            through = lax.dynamic_update_slice_in_dim(through, part, (spot ^ m) * quarter, 0)
    with jax.named_scope("unpack"):
        assembled = pl.pallas_call(
            lambda *refs: unpack_kernel(face_dev, *refs),
            out_shape=jax.ShapeDtypeStruct((rhs_count, face_dev * width), F32),
            name="unpack",
        )(got, face_rhs[0])
    with jax.named_scope("source"):
        high = assembled.astype(BF)
        low = (assembled - high.astype(F32)).astype(BF)
        both = jnp.dot(
            jnp.concatenate([high, low], axis=0), outward, preferred_element_type=F32
        )
        source = both[:rhs_count] + both[rhs_count:]

    with jax.named_scope("sum_source"):
        part = source.astype(BF)
        part = total([part] + [exchange(part, m, 0) for m in range(1, x_count)]).astype(BF)
        part = total([part] + [exchange(part, 0, m) for m in range(1, four)]).astype(BF)
        source = total([part, exchange(part, 0, far)])
        source_slab = lax.dynamic_slice_in_dim(source, here_x * slab, slab, 1)
        source_once = jnp.where(here_x == 0, source, 0.0)
    panel = None
    for layer in range(sweep_count - 1):
        with jax.named_scope("stage%d" % layer):
            if layer % 2 == 0:
                following = source_slab
                if panel is not None:
                    following = source_slab - lax.dot_general(
                        panel, through, (((1,), (1,)), ((), ())), preferred_element_type=F32
                    )
                panel_slab = exchange(following.astype(BF), 0, 0, 1, 0, 2)
            else:
                part = source_once - jnp.dot(panel_slab, through, preferred_element_type=F32)
                part = part.astype(BF)
                panel = total(
                    [exchange(part, m, 0, 1, 1, 2) for m in range(x_count)]
                ).astype(BF)
    with jax.named_scope("spread"):
        spread = jnp.zeros((rhs_count, panel_size), BF)
        for m in range(x_count):
            part = panel_slab if m == 0 else exchange(panel_slab, m, 0)
            spread = lax.dynamic_update_slice_in_dim(spread, part, (here_x ^ m) * slab, 1)
        panel = jnp.where(odd, spread, panel)
    with jax.named_scope("solve"):
        coupled = jnp.dot(panel, coupling_in, preferred_element_type=F32)
        local = (assembled - coupled).astype(BF).reshape(rhs_count, face_dev, width)
        solved = jnp.einsum("rfw,fwv->rfv", local, inverse, preferred_element_type=F32)
    return solved[None]


def solution(mesh):
    shape = (mesh.shape["sweep"], 8, mesh.shape["layer"] // 8)
    fine = Mesh(mesh.devices.reshape(shape), ("sweep", "z", "x"))
    layer = ("z", "x")
    everywhere = ("sweep", "z", "x")
    return jax.shard_map(
        lambda *args: on_device(shape, *args),
        mesh=fine,
        in_specs=(
            P("sweep", None, layer, None),
            P(everywhere, None),
            P(everywhere, None),
            P(everywhere),
            P("sweep", layer, None, None),
            P("sweep", None, layer),
            P("sweep", layer, None),
        ),
        out_specs=P("sweep", None, layer, None),
        check_vma=False,
    )
```

```python
import jax
import jax.numpy as jnp
from jax import lax
from jax.experimental import pallas as pl
from jax.experimental.pallas import tpu as pltpu
from jax.sharding import Mesh
from jax.sharding import PartitionSpec as P

BF = jnp.bfloat16
F32 = jnp.float32
LANES = 128
FIRST = 2


def pack_kernel(owner_count, owner_ref, slot_ref, rows_ref, out_ref):
    row_total, width = rows_ref.shape
    capacity = row_total // owner_count * 2
    owner = owner_ref[...]
    match = (lax.broadcasted_iota(jnp.int32, (owner_count, row_total), 0) == owner).astype(F32)
    earlier_mask = (
        lax.broadcasted_iota(jnp.int32, (row_total, row_total), 0)
        < lax.broadcasted_iota(jnp.int32, (row_total, row_total), 1)
    )
    earlier = jnp.dot(
        match.astype(BF), earlier_mask.astype(F32).astype(BF), preferred_element_type=F32
    )
    position = jnp.sum(earlier * match, axis=0, keepdims=True).astype(jnp.int32)
    target = owner * capacity + position
    slots = (slot_ref[...] + 1).astype(F32)
    rows = rows_ref[...].astype(BF)
    block = 256
    for start in range(0, owner_count * capacity, block):
        place = lax.broadcasted_iota(jnp.int32, (block, row_total), 0) + start
        chosen = place == target
        picked = jnp.where(chosen, 1.0, 0.0).astype(BF)
        out_ref[pl.ds(start, block), pl.ds(0, width)] = jnp.dot(
            picked, rows, preferred_element_type=F32
        ).astype(BF)
        slot = jnp.sum(jnp.where(chosen, slots, 0.0), axis=1, keepdims=True)
        out_ref[pl.ds(start, block), pl.ds(width, LANES)] = jnp.broadcast_to(
            slot, (block, LANES)
        ).astype(BF)


def source_kernel(face_dev, got_ref, face_ref, outward_ref, assembled_ref, source_ref):
    rhs_count = assembled_ref.shape[0]
    width = assembled_ref.shape[1] // face_dev
    slot = got_ref[:, pl.ds(width, LANES)].astype(F32)
    lane = lax.broadcasted_iota(jnp.int32, slot.shape, 1)
    wanted = (lane % rhs_count) * face_dev + lane // rhs_count + 1
    wanted = jnp.where(lane < rhs_count * face_dev, wanted, -1).astype(F32)
    picked = jnp.where(slot == wanted, 1.0, 0.0).astype(BF)
    summed = lax.dot_general(
        picked,
        got_ref[:, pl.ds(0, width)],
        (((0,), (0,)), ((), ())),
        preferred_element_type=F32,
    )
    for face in range(face_dev):
        assembled_ref[:, pl.ds(face * width, width)] = (
            face_ref[:, face, :] + summed[face * rhs_count : (face + 1) * rhs_count, :]
        )
    assembled = assembled_ref[...]
    high = assembled.astype(BF)
    low = (assembled - high.astype(F32)).astype(BF)
    both = jnp.dot(
        jnp.concatenate([high, low], axis=0), outward_ref[...], preferred_element_type=F32
    )
    source_ref[...] = both[:rhs_count] + both[rhs_count:]


def outward_kernel(face_dev, side_ref, inv_ref, out_ref, in_ref, outward_ref, piece_ref, held):
    step = pl.program_id(0)
    width = inv_ref.shape[1]

    @pl.when(step < face_dev)
    def _():
        rows = jnp.dot(inv_ref[0], out_ref[...], preferred_element_type=F32).astype(BF)
        outward_ref[...] = rows
        held[pl.ds(pl.multiple_of(step * width, width), width), :] = rows

    @pl.when(step >= face_dev)
    def _():
        block = jnp.where(side_ref[1] == 1, step - face_dev, side_ref[0] ^ FIRST)
        slab = piece_ref.shape[1]
        columns = held[:, pl.ds(pl.multiple_of(block * slab, slab), slab)]
        piece_ref[...] = jnp.dot(in_ref[...], columns, preferred_element_type=F32).astype(BF)


def fold_kernel(side_ref, in_ref, outward_ref, piece_ref):
    piece_ref[0] = jnp.dot(
        in_ref[...], outward_ref[...], preferred_element_type=F32
    ).astype(BF)


def on_device(shape, face_rhs, res_rows, row_owner, row_slot, inv_blocks, couple_in, couple_out):
    sweep_count, z_count, x_count = shape
    group_size = z_count * x_count
    rhs_count, face_dev, width = face_rhs.shape[1:]
    row_total = res_rows.shape[0]
    capacity = 2 * row_total // group_size
    coupling_in, coupling_out, inverse = couple_in[0], couple_out[0], inv_blocks[0]

    def number(s, z, x):
        return (s * z_count + z) * x_count + x

    def exchange(value, mask_x, mask_z=0, partner=lambda s: s, along_z=None):
        pairs = [
            (
                number(s, z, x),
                number(partner(s), along_z[z] if along_z else z ^ mask_z, x ^ mask_x),
            )
            for s in range(sweep_count)
            for z in range(z_count)
            for x in range(x_count)
        ]
        return lax.ppermute(value, ("sweep", "z", "x"), pairs)

    def after_even(s):
        return s ^ 1

    def after_odd(s):
        return (s + 1 if s % 2 else s - 1) % sweep_count

    def total(values):
        result = values[0].astype(F32)
        for value in values[1:]:
            result = result + value.astype(F32)
        return result

    far, four = z_count - 1, z_count // 2
    here_x, here_z = lax.axis_index("x"), lax.axis_index("z")
    own_layer = lax.axis_index("sweep")
    odd = own_layer % 2 == 1
    panel_size = coupling_in.shape[0]
    slab = panel_size // x_count

    with jax.named_scope("pack"):
        packed = pl.pallas_call(
            lambda *refs: pack_kernel(group_size, *refs),
            out_shape=jax.ShapeDtypeStruct((group_size * capacity, width + LANES), BF),
            name="pack",
        )(row_owner.reshape(1, row_total), row_slot.reshape(1, row_total), res_rows)
    with jax.named_scope("route"):
        inverse_later, packed = lax.optimization_barrier((inverse, packed))
        got = lax.all_to_all(
            packed.reshape(group_size, capacity, width + LANES),
            ("z", "x"),
            split_axis=0,
            concat_axis=0,
            tiled=True,
        ).reshape(group_size * capacity, width + LANES)
    with jax.named_scope("fold"):
        side = jnp.stack([here_x, odd.astype(jnp.int32)])
        faces = panel_size // slab

        def mask_of(turn):
            return jnp.where(turn == 0, 1, jnp.where(turn == 1, 3, 0))

        outward, piece2 = pl.pallas_call(
            lambda *refs: outward_kernel(face_dev, *refs),
            grid_spec=pltpu.PrefetchScalarGridSpec(
                num_scalar_prefetch=1,
                grid=(face_dev + faces,),
                in_specs=[
                    pl.BlockSpec(
                        (1, width, width), lambda i, side: (jnp.minimum(i, face_dev - 1), 0, 0)
                    ),
                    pl.BlockSpec(
                        (width, panel_size), lambda i, side: (jnp.minimum(i, face_dev - 1), 0)
                    ),
                    pl.BlockSpec(
                        (slab, face_dev * width),
                        lambda i, side: (
                            jnp.where(
                                side[1] == 1, side[0] ^ FIRST, jnp.maximum(i - face_dev, 0)
                            ),
                            0,
                        ),
                    ),
                ],
                out_specs=[
                    pl.BlockSpec(
                        (width, panel_size), lambda i, side: (jnp.minimum(i, face_dev - 1), 0)
                    ),
                    pl.BlockSpec(
                        (slab, slab), lambda i, side: (0, jnp.maximum(i - face_dev, 0))
                    ),
                ],
                scratch_shapes=[pltpu.VMEM((face_dev * width, panel_size), BF)],
            ),
            out_shape=[
                jax.ShapeDtypeStruct((face_dev * width, panel_size), BF),
                jax.ShapeDtypeStruct((slab, panel_size), BF),
            ],
            compiler_params=pltpu.CompilerParams(vmem_limit_bytes=40 << 20),
            name="outward",
        )(side, inverse_later, coupling_out, coupling_in)
        pieces = pl.pallas_call(
            fold_kernel,
            grid_spec=pltpu.PrefetchScalarGridSpec(
                num_scalar_prefetch=1,
                grid=(x_count - 1, faces),
                in_specs=[
                    pl.BlockSpec(
                        (slab, face_dev * width),
                        lambda i, j, side: (
                            jnp.where(side[1] == 1, side[0] ^ mask_of(i), j),
                            0,
                        ),
                    ),
                    pl.BlockSpec(
                        (face_dev * width, slab),
                        lambda i, j, side: (
                            0,
                            jnp.where(side[1] == 1, j, side[0] ^ mask_of(i)),
                        ),
                    ),
                ],
                out_specs=pl.BlockSpec((1, slab, slab), lambda i, j, side: (i, 0, j)),
            ),
            out_shape=jax.ShapeDtypeStruct((x_count - 1, slab, panel_size), BF),
            compiler_params=pltpu.CompilerParams(vmem_limit_bytes=40 << 20),
            name="fold",
        )(side, coupling_in, outward)
        piece1, piece3, piece0 = pieces[0], pieces[1], pieces[2]
    with jax.named_scope("sum_x"):
        half = slab // 2
        upper = exchange(piece2[:half], 1)
        lower = exchange(piece2[half:], 3)
        to3 = jnp.concatenate([total([piece3[:half], upper]).astype(BF), piece3[half:]], axis=0)
        to1 = jnp.concatenate([piece1[:half], total([piece1[half:], lower]).astype(BF)], axis=0)
        got, to3, to1 = lax.optimization_barrier((got, to3, to1))
        summed_x = total(
            [piece0, exchange(to3, 3), exchange(to1, 1)]
        ).astype(BF)
    with jax.named_scope("source"):
        vmem = pl.BlockSpec(memory_space=pltpu.VMEM)
        assembled, source = pl.pallas_call(
            lambda *refs: source_kernel(face_dev, *refs),
            in_specs=[vmem, vmem, vmem],
            out_specs=[vmem, vmem],
            out_shape=[jax.ShapeDtypeStruct((rhs_count, face_dev * width), F32)] * 2,
            name="source",
        )(got, face_rhs[0], outward)
    with jax.named_scope("sum_source"):
        part = source.astype(BF)
        part = total([part] + [exchange(part, m) for m in range(1, x_count)]).astype(BF)
        source_x, summed_x = lax.optimization_barrier((part, summed_x))
    with jax.named_scope("sum_z"):
        turns = [z ^ 1 for z in range(z_count)], [3, 6, 5, 0, 7, 2, 1, 4]

        def shifted(places):
            return [(places[(z + 1) % z_count] - 1) % z_count for z in range(z_count)]

        near, across = turns
        paths = [(near, shifted(near), across), (shifted(near), near, shifted(across))]
        part_rows = slab // 2
        bits = [((102 >> z) & 1, (180 >> z) & 1) for z in (here_z, (here_z + 1) % z_count)]
        summed = [summed_x[:part_rows], summed_x[part_rows:]]

        def halved(rows, bit):
            size = rows.shape[0] // 2
            kept = lax.dynamic_slice_in_dim(rows, bit * size, size, 0)
            given = lax.dynamic_slice_in_dim(rows, (1 - bit) * size, size, 0)
            return kept, given

        def joined(own, other, bit):
            size = own.shape[0]
            both = jnp.concatenate([own, own], axis=0)
            return lax.dynamic_update_slice_in_dim(both, other, (1 - bit) * size, 0)

        def swap(values, turn):
            return [exchange(v, 0, 0, along_z=p[turn]) for v, p in zip(values, paths)]

        for turn in range(2):
            split = [halved(rows, bit[turn]) for rows, bit in zip(summed, bits)]
            got_rows = swap([given for _, given in split], turn)
            summed = [total([kept, new]).astype(BF) for (kept, _), new in zip(split, got_rows)]
            if turn == 0:
                source_x, summed[0] = lax.optimization_barrier((source_x, summed[0]))
                source_z = [source_x] + [exchange(source_x, 0, m) for m in range(1, four)]
            else:
                source_z = total(source_z).astype(BF)
                source_z, summed[0] = lax.optimization_barrier((source_z, summed[0]))
                source_far = exchange(source_z, 0, far)
        summed = [total([rows, new]).astype(BF) for rows, new in zip(summed, swap(summed, 2))]
        for turn in (1, 0):
            got_rows = swap(summed, turn)
            summed = [
                joined(rows, new, bit[turn]) for rows, new, bit in zip(summed, got_rows, bits)
            ]
        through = jnp.concatenate(summed, axis=0)
        source = total([source_z, source_far])
        source_slab = lax.dynamic_slice_in_dim(source, here_x * slab, slab, 1)
        source_once = jnp.where(here_x == 0, source, 0.0)
    through_columns = jnp.concatenate(
        [through[:, start : start + slab] for start in range(0, panel_size, slab)], axis=0
    )
    panel = None
    for layer in range(sweep_count - 1):
        with jax.named_scope("stage%d" % layer):
            if layer % 2 == 0:
                following = source_slab
                if panel is not None:
                    following = source_slab - jnp.dot(
                        panel, through_columns, preferred_element_type=F32
                    )
                following = following.astype(BF)
                if layer < sweep_count - 2:
                    panel_slab = exchange(following, 0, 0, after_even)
            else:
                part = source_once - jnp.dot(panel_slab, through, preferred_element_type=F32)
                part = part.astype(BF)
                part = total([exchange(part, m, 0, after_odd) for m in range(x_count)])
                panel = jnp.where(own_layer == 0, 0.0, part).astype(BF)
    with jax.named_scope("spread"):
        spread = jnp.zeros((rhs_count, panel_size), BF)
        for m in range(x_count):
            part = exchange(following, m, 0, after_even)
            spread = lax.dynamic_update_slice_in_dim(spread, part, (here_x ^ m) * slab, 1)
        panel = jnp.where(odd, spread, panel)
    with jax.named_scope("solve"):
        coupled = jnp.dot(panel, coupling_in, preferred_element_type=F32)
        local = (assembled - coupled).astype(BF).reshape(rhs_count, face_dev, width)
        solved = jnp.einsum("rfw,fwv->rfv", local, inverse, preferred_element_type=F32)
    return solved[None]


def solution(mesh):
    shape = (mesh.shape["sweep"], 8, mesh.shape["layer"] // 8)
    fine = Mesh(mesh.devices.reshape(shape), ("sweep", "z", "x"))
    layer = ("z", "x")
    everywhere = ("sweep", "z", "x")
    return jax.shard_map(
        lambda *args: on_device(shape, *args),
        mesh=fine,
        in_specs=(
            P("sweep", None, layer, None),
            P(everywhere, None),
            P(everywhere, None),
            P(everywhere),
            P("sweep", layer, None, None),
            P("sweep", None, layer),
            P("sweep", layer, None),
        ),
        out_specs=P("sweep", None, layer, None),
        check_vma=False,
    )
```

```python
import jax
import jax.numpy as jnp
from jax import lax
from jax.experimental import pallas as pl
from jax.experimental.pallas import tpu as pltpu
from jax.sharding import Mesh
from jax.sharding import PartitionSpec as P

BF = jnp.bfloat16
F32 = jnp.float32
LANES = 128
FIRST = 2


def pack_kernel(owner_count, owner_ref, slot_ref, rows_ref, out_ref):
    row_total, width = rows_ref.shape
    capacity = row_total // owner_count * 2
    owner = owner_ref[...]
    match = (lax.broadcasted_iota(jnp.int32, (owner_count, row_total), 0) == owner).astype(F32)
    earlier_mask = (
        lax.broadcasted_iota(jnp.int32, (row_total, row_total), 0)
        < lax.broadcasted_iota(jnp.int32, (row_total, row_total), 1)
    )
    earlier = jnp.dot(
        match.astype(BF), earlier_mask.astype(F32).astype(BF), preferred_element_type=F32
    )
    position = jnp.sum(earlier * match, axis=0, keepdims=True).astype(jnp.int32)
    target = owner * capacity + position
    slots = (slot_ref[...] + 1).astype(F32)
    rows = rows_ref[...].astype(BF)
    block = 256
    for start in range(0, owner_count * capacity, block):
        place = lax.broadcasted_iota(jnp.int32, (block, row_total), 0) + start
        chosen = place == target
        picked = jnp.where(chosen, 1.0, 0.0).astype(BF)
        out_ref[pl.ds(start, block), pl.ds(0, width)] = jnp.dot(
            picked, rows, preferred_element_type=F32
        ).astype(BF)
        slot = jnp.sum(jnp.where(chosen, slots, 0.0), axis=1, keepdims=True)
        out_ref[pl.ds(start, block), pl.ds(width, LANES)] = jnp.broadcast_to(
            slot, (block, LANES)
        ).astype(BF)


def source_kernel(face_dev, got_ref, face_ref, outward_ref, assembled_ref, source_ref):
    rhs_count = assembled_ref.shape[0]
    width = assembled_ref.shape[1] // face_dev
    slot = got_ref[:, pl.ds(width, LANES)].astype(F32)
    lane = lax.broadcasted_iota(jnp.int32, slot.shape, 1)
    wanted = (lane % rhs_count) * face_dev + lane // rhs_count + 1
    wanted = jnp.where(lane < rhs_count * face_dev, wanted, -1).astype(F32)
    picked = jnp.where(slot == wanted, 1.0, 0.0).astype(BF)
    summed = lax.dot_general(
        picked,
        got_ref[:, pl.ds(0, width)],
        (((0,), (0,)), ((), ())),
        preferred_element_type=F32,
    )
    for face in range(face_dev):
        assembled_ref[:, pl.ds(face * width, width)] = (
            face_ref[:, face, :] + summed[face * rhs_count : (face + 1) * rhs_count, :]
        )
    assembled = assembled_ref[...]
    high = assembled.astype(BF)
    low = (assembled - high.astype(F32)).astype(BF)
    both = jnp.dot(
        jnp.concatenate([high, low], axis=0), outward_ref[...], preferred_element_type=F32
    )
    source_ref[...] = both[:rhs_count] + both[rhs_count:]


def outward_kernel(face_dev, side_ref, inv_ref, out_ref, in_ref, outward_ref, piece_ref, held):
    step = pl.program_id(0)
    width = inv_ref.shape[1]

    @pl.when(step < face_dev)
    def _():
        rows = jnp.dot(inv_ref[0], out_ref[...], preferred_element_type=F32).astype(BF)
        outward_ref[...] = rows
        held[pl.ds(pl.multiple_of(step * width, width), width), :] = rows

    @pl.when(step >= face_dev)
    def _():
        block = jnp.where(side_ref[1] == 1, step - face_dev, side_ref[0] ^ FIRST)
        slab = piece_ref.shape[1]
        columns = held[:, pl.ds(pl.multiple_of(block * slab, slab), slab)]
        piece_ref[...] = jnp.dot(in_ref[...], columns, preferred_element_type=F32).astype(BF)


def fold_kernel(side_ref, in_ref, outward_ref, piece_ref):
    piece_ref[0] = jnp.dot(
        in_ref[...], outward_ref[...], preferred_element_type=F32
    ).astype(BF)


def on_device(shape, face_rhs, res_rows, row_owner, row_slot, inv_blocks, couple_in, couple_out):
    sweep_count, z_count, x_count = shape
    group_size = z_count * x_count
    rhs_count, face_dev, width = face_rhs.shape[1:]
    row_total = res_rows.shape[0]
    capacity = 2 * row_total // group_size
    coupling_in, coupling_out, inverse = couple_in[0], couple_out[0], inv_blocks[0]

    def number(s, z, x):
        return (s * z_count + z) * x_count + x

    def exchange(value, mask_x, mask_z=0, partner=lambda s: s, along_z=None):
        pairs = [
            (
                number(s, z, x),
                number(partner(s), along_z[z] if along_z else z ^ mask_z, x ^ mask_x),
            )
            for s in range(sweep_count)
            for z in range(z_count)
            for x in range(x_count)
        ]
        return lax.ppermute(value, ("sweep", "z", "x"), pairs)

    def after_even(s):
        return s ^ 1

    def after_odd(s):
        return (s + 1 if s % 2 else s - 1) % sweep_count

    def total(values):
        result = values[0].astype(F32)
        for value in values[1:]:
            result = result + value.astype(F32)
        return result

    far, four = z_count - 1, z_count // 2
    here_x, here_z = lax.axis_index("x"), lax.axis_index("z")
    own_layer = lax.axis_index("sweep")
    odd = own_layer % 2 == 1
    panel_size = coupling_in.shape[0]
    slab = panel_size // x_count

    with jax.named_scope("pack"):
        packed = pl.pallas_call(
            lambda *refs: pack_kernel(group_size, *refs),
            out_shape=jax.ShapeDtypeStruct((group_size * capacity, width + LANES), BF),
            name="pack",
        )(row_owner.reshape(1, row_total), row_slot.reshape(1, row_total), res_rows)
    with jax.named_scope("route"):
        inverse_later, packed = lax.optimization_barrier((inverse, packed))
        got = lax.all_to_all(
            packed.reshape(group_size, capacity, width + LANES),
            ("z", "x"),
            split_axis=0,
            concat_axis=0,
            tiled=True,
        ).reshape(group_size * capacity, width + LANES)
    with jax.named_scope("fold"):
        side = jnp.stack([here_x, odd.astype(jnp.int32)])
        faces = panel_size // slab

        def mask_of(turn):
            return jnp.where(turn == 0, 1, jnp.where(turn == 1, 3, 0))

        outward, piece2 = pl.pallas_call(
            lambda *refs: outward_kernel(face_dev, *refs),
            grid_spec=pltpu.PrefetchScalarGridSpec(
                num_scalar_prefetch=1,
                grid=(face_dev + faces,),
                in_specs=[
                    pl.BlockSpec(
                        (1, width, width), lambda i, side: (jnp.minimum(i, face_dev - 1), 0, 0)
                    ),
                    pl.BlockSpec(
                        (width, panel_size), lambda i, side: (jnp.minimum(i, face_dev - 1), 0)
                    ),
                    pl.BlockSpec(
                        (slab, face_dev * width),
                        lambda i, side: (
                            jnp.where(
                                side[1] == 1, side[0] ^ FIRST, jnp.maximum(i - face_dev, 0)
                            ),
                            0,
                        ),
                    ),
                ],
                out_specs=[
                    pl.BlockSpec(
                        (width, panel_size), lambda i, side: (jnp.minimum(i, face_dev - 1), 0)
                    ),
                    pl.BlockSpec(
                        (slab, slab), lambda i, side: (0, jnp.maximum(i - face_dev, 0))
                    ),
                ],
                scratch_shapes=[pltpu.VMEM((face_dev * width, panel_size), BF)],
            ),
            out_shape=[
                jax.ShapeDtypeStruct((face_dev * width, panel_size), BF),
                jax.ShapeDtypeStruct((slab, panel_size), BF),
            ],
            compiler_params=pltpu.CompilerParams(vmem_limit_bytes=40 << 20),
            name="outward",
        )(side, inverse_later, coupling_out, coupling_in)
        pieces = pl.pallas_call(
            fold_kernel,
            grid_spec=pltpu.PrefetchScalarGridSpec(
                num_scalar_prefetch=1,
                grid=(x_count - 1, faces),
                in_specs=[
                    pl.BlockSpec(
                        (slab, face_dev * width),
                        lambda i, j, side: (
                            jnp.where(side[1] == 1, side[0] ^ mask_of(i), j),
                            0,
                        ),
                    ),
                    pl.BlockSpec(
                        (face_dev * width, slab),
                        lambda i, j, side: (
                            0,
                            jnp.where(side[1] == 1, j, side[0] ^ mask_of(i)),
                        ),
                    ),
                ],
                out_specs=pl.BlockSpec((1, slab, slab), lambda i, j, side: (i, 0, j)),
            ),
            out_shape=jax.ShapeDtypeStruct((x_count - 1, slab, panel_size), BF),
            compiler_params=pltpu.CompilerParams(vmem_limit_bytes=40 << 20),
            name="fold",
        )(side, coupling_in, outward)
        piece1, piece3, piece0 = pieces[0], pieces[1], pieces[2]
    with jax.named_scope("sum_x"):
        half = slab // 2
        upper = exchange(piece2[:half], 1)
        lower = exchange(piece2[half:], 3)
        to3 = jnp.concatenate([total([piece3[:half], upper]).astype(BF), piece3[half:]], axis=0)
        to1 = jnp.concatenate([piece1[:half], total([piece1[half:], lower]).astype(BF)], axis=0)
        got, to3, to1 = lax.optimization_barrier((got, to3, to1))
        summed_x = total(
            [piece0, exchange(to3, 3), exchange(to1, 1)]
        ).astype(BF)
    with jax.named_scope("source"):
        vmem = pl.BlockSpec(memory_space=pltpu.VMEM)
        assembled, source = pl.pallas_call(
            lambda *refs: source_kernel(face_dev, *refs),
            in_specs=[vmem, vmem, vmem],
            out_specs=[vmem, vmem],
            out_shape=[jax.ShapeDtypeStruct((rhs_count, face_dev * width), F32)] * 2,
            name="source",
        )(got, face_rhs[0], outward)
    with jax.named_scope("sum_source"):
        part = source.astype(BF)
        part = total([part] + [exchange(part, 0, m) for m in range(1, four)]).astype(BF)
        part = total([part, exchange(part, 0, far)]).astype(BF)
        source_parts = [part] + [exchange(part, m) for m in range(1, x_count)]
    with jax.named_scope("sum_z"):
        turns = [z ^ 1 for z in range(z_count)], [3, 6, 5, 0, 7, 2, 1, 4]

        def shifted(places):
            return [(places[(z + 1) % z_count] - 1) % z_count for z in range(z_count)]

        near, across = turns
        paths = [(near, shifted(near), across), (shifted(near), near, shifted(across))]
        part_rows = slab // 2
        bits = [((102 >> z) & 1, (180 >> z) & 1) for z in (here_z, (here_z + 1) % z_count)]
        summed = [summed_x[:part_rows], summed_x[part_rows:]]

        def halved(rows, bit):
            size = rows.shape[0] // 2
            kept = lax.dynamic_slice_in_dim(rows, bit * size, size, 0)
            given = lax.dynamic_slice_in_dim(rows, (1 - bit) * size, size, 0)
            return kept, given

        def joined(own, other, bit):
            size = own.shape[0]
            both = jnp.concatenate([own, own], axis=0)
            return lax.dynamic_update_slice_in_dim(both, other, (1 - bit) * size, 0)

        def swap(values, turn):
            return [exchange(v, 0, 0, along_z=p[turn]) for v, p in zip(values, paths)]

        for turn in range(2):
            split = [halved(rows, bit[turn]) for rows, bit in zip(summed, bits)]
            got_rows = swap([given for _, given in split], turn)
            summed = [total([kept, new]).astype(BF) for (kept, _), new in zip(split, got_rows)]
            if turn == 0:
                source, summed[0] = lax.optimization_barrier((total(source_parts), summed[0]))
        summed = [total([rows, new]).astype(BF) for rows, new in zip(summed, swap(summed, 2))]
        for turn in (1, 0):
            got_rows = swap(summed, turn)
            summed = [
                joined(rows, new, bit[turn]) for rows, new, bit in zip(summed, got_rows, bits)
            ]
        through = jnp.concatenate(summed, axis=0)
        source_slab = lax.dynamic_slice_in_dim(source, here_x * slab, slab, 1)
        source_once = jnp.where(here_x == 0, source, 0.0)
    through_columns = jnp.concatenate(
        [through[:, start : start + slab] for start in range(0, panel_size, slab)], axis=0
    )
    panel = None
    for layer in range(sweep_count - 1):
        with jax.named_scope("stage%d" % layer):
            if layer % 2 == 0:
                following = source_slab
                if panel is not None:
                    following = source_slab - jnp.dot(
                        panel, through_columns, preferred_element_type=F32
                    )
                following = following.astype(BF)
                if layer < sweep_count - 2:
                    panel_slab = exchange(following, 0, 0, after_even)
            else:
                part = source_once - jnp.dot(panel_slab, through, preferred_element_type=F32)
                part = part.astype(BF)
                part = total([exchange(part, m, 0, after_odd) for m in range(x_count)])
                panel = jnp.where(own_layer == 0, 0.0, part).astype(BF)
    with jax.named_scope("spread"):
        spread = jnp.zeros((rhs_count, panel_size), BF)
        for m in range(x_count):
            part = exchange(following, m, 0, after_even)
            spread = lax.dynamic_update_slice_in_dim(spread, part, (here_x ^ m) * slab, 1)
        panel = jnp.where(odd, spread, panel)
    with jax.named_scope("solve"):
        coupled = jnp.dot(panel, coupling_in, preferred_element_type=F32)
        local = (assembled - coupled).astype(BF).reshape(rhs_count, face_dev, width)
        solved = jnp.einsum("rfw,fwv->rfv", local, inverse, preferred_element_type=F32)
    return solved[None]


def solution(mesh):
    shape = (mesh.shape["sweep"], 8, mesh.shape["layer"] // 8)
    fine = Mesh(mesh.devices.reshape(shape), ("sweep", "z", "x"))
    layer = ("z", "x")
    everywhere = ("sweep", "z", "x")
    return jax.shard_map(
        lambda *args: on_device(shape, *args),
        mesh=fine,
        in_specs=(
            P("sweep", None, layer, None),
            P(everywhere, None),
            P(everywhere, None),
            P(everywhere),
            P("sweep", layer, None, None),
            P("sweep", None, layer),
            P("sweep", layer, None),
        ),
        out_specs=P("sweep", None, layer, None),
        check_vma=False,
    )
```

```python
import jax
import jax.numpy as jnp
from jax import lax
from jax.experimental import pallas as pl
from jax.experimental.pallas import tpu as pltpu
from jax.sharding import Mesh
from jax.sharding import PartitionSpec as P

BF = jnp.bfloat16
F32 = jnp.float32
LANES = 128
FIRST = 2


def pack_kernel(owner_count, owner_ref, slot_ref, rows_ref, out_ref):
    row_total, width = rows_ref.shape
    capacity = row_total // owner_count * 2
    owner = owner_ref[...]
    match = (lax.broadcasted_iota(jnp.int32, (owner_count, row_total), 0) == owner).astype(F32)
    earlier_mask = (
        lax.broadcasted_iota(jnp.int32, (row_total, row_total), 0)
        < lax.broadcasted_iota(jnp.int32, (row_total, row_total), 1)
    )
    earlier = jnp.dot(
        match.astype(BF), earlier_mask.astype(F32).astype(BF), preferred_element_type=F32
    )
    position = jnp.sum(earlier * match, axis=0, keepdims=True).astype(jnp.int32)
    target = owner * capacity + position
    slots = (slot_ref[...] + 1).astype(F32)
    rows = rows_ref[...].astype(BF)
    block = 256
    for start in range(0, owner_count * capacity, block):
        place = lax.broadcasted_iota(jnp.int32, (block, row_total), 0) + start
        chosen = place == target
        picked = jnp.where(chosen, 1.0, 0.0).astype(BF)
        out_ref[pl.ds(start, block), pl.ds(0, width)] = jnp.dot(
            picked, rows, preferred_element_type=F32
        ).astype(BF)
        slot = jnp.sum(jnp.where(chosen, slots, 0.0), axis=1, keepdims=True)
        out_ref[pl.ds(start, block), pl.ds(width, LANES)] = jnp.broadcast_to(
            slot, (block, LANES)
        ).astype(BF)


def source_kernel(face_dev, got_ref, face_ref, outward_ref, assembled_ref, source_ref):
    rhs_count = assembled_ref.shape[0]
    width = assembled_ref.shape[1] // face_dev
    slot = got_ref[:, pl.ds(width, LANES)].astype(F32)
    lane = lax.broadcasted_iota(jnp.int32, slot.shape, 1)
    wanted = (lane % rhs_count) * face_dev + lane // rhs_count + 1
    wanted = jnp.where(lane < rhs_count * face_dev, wanted, -1).astype(F32)
    picked = jnp.where(slot == wanted, 1.0, 0.0).astype(BF)
    summed = lax.dot_general(
        picked,
        got_ref[:, pl.ds(0, width)],
        (((0,), (0,)), ((), ())),
        preferred_element_type=F32,
    )
    for face in range(face_dev):
        assembled_ref[:, pl.ds(face * width, width)] = (
            face_ref[:, face, :] + summed[face * rhs_count : (face + 1) * rhs_count, :]
        )
    assembled = assembled_ref[...]
    high = assembled.astype(BF)
    low = (assembled - high.astype(F32)).astype(BF)
    both = jnp.dot(
        jnp.concatenate([high, low], axis=0), outward_ref[...], preferred_element_type=F32
    )
    source_ref[...] = both[:rhs_count] + both[rhs_count:]


def outward_kernel(face_dev, side_ref, inv_ref, out_ref, in_ref, outward_ref, piece_ref, held):
    step = pl.program_id(0)
    width = inv_ref.shape[1]

    @pl.when(step < face_dev)
    def _():
        rows = jnp.dot(inv_ref[0], out_ref[...], preferred_element_type=F32).astype(BF)
        outward_ref[...] = rows
        held[pl.ds(pl.multiple_of(step * width, width), width), :] = rows

    @pl.when(step >= face_dev)
    def _():
        block = jnp.where(side_ref[1] == 1, step - face_dev, side_ref[0] ^ FIRST)
        slab = piece_ref.shape[1]
        columns = held[:, pl.ds(pl.multiple_of(block * slab, slab), slab)]
        piece_ref[...] = jnp.dot(in_ref[...], columns, preferred_element_type=F32).astype(BF)


def fold_kernel(side_ref, in_ref, outward_ref, piece_ref):
    piece_ref[0] = jnp.dot(
        in_ref[...], outward_ref[...], preferred_element_type=F32
    ).astype(BF)


def solve_kernel(panel_ref, in_ref, assembled_ref, inv_ref, out_ref):
    coupled = jnp.dot(panel_ref[...], in_ref[...], preferred_element_type=F32)
    local = (assembled_ref[...] - coupled).astype(BF)
    width = inv_ref.shape[1]
    for face in range(inv_ref.shape[0]):
        out_ref[:, face, :] = jnp.dot(
            local[:, face * width : (face + 1) * width], inv_ref[face], preferred_element_type=F32
        )


def on_device(shape, face_rhs, res_rows, row_owner, row_slot, inv_blocks, couple_in, couple_out):
    sweep_count, z_count, x_count = shape
    group_size = z_count * x_count
    rhs_count, face_dev, width = face_rhs.shape[1:]
    row_total = res_rows.shape[0]
    capacity = 2 * row_total // group_size
    coupling_in, coupling_out, inverse = couple_in[0], couple_out[0], inv_blocks[0]

    def number(s, z, x):
        return (s * z_count + z) * x_count + x

    def exchange(value, mask_x, mask_z=0, partner=lambda s: s, along_z=None):
        pairs = [
            (
                number(s, z, x),
                number(partner(s), along_z[z] if along_z else z ^ mask_z, x ^ mask_x),
            )
            for s in range(sweep_count)
            for z in range(z_count)
            for x in range(x_count)
        ]
        return lax.ppermute(value, ("sweep", "z", "x"), pairs)

    def after_even(s):
        return s ^ 1

    def after_odd(s):
        return (s + 1 if s % 2 else s - 1) % sweep_count

    def total(values):
        result = values[0].astype(F32)
        for value in values[1:]:
            result = result + value.astype(F32)
        return result

    far, four = z_count - 1, z_count // 2
    here_x, here_z = lax.axis_index("x"), lax.axis_index("z")
    own_layer = lax.axis_index("sweep")
    odd = own_layer % 2 == 1
    panel_size = coupling_in.shape[0]
    slab = panel_size // x_count

    with jax.named_scope("pack"):
        packed = pl.pallas_call(
            lambda *refs: pack_kernel(group_size, *refs),
            out_shape=jax.ShapeDtypeStruct((group_size * capacity, width + LANES), BF),
            name="pack",
        )(row_owner.reshape(1, row_total), row_slot.reshape(1, row_total), res_rows)
    with jax.named_scope("route"):
        inverse_later, packed = lax.optimization_barrier((inverse, packed))
        got = lax.all_to_all(
            packed.reshape(group_size, capacity, width + LANES),
            ("z", "x"),
            split_axis=0,
            concat_axis=0,
            tiled=True,
        ).reshape(group_size * capacity, width + LANES)
    with jax.named_scope("fold"):
        side = jnp.stack([here_x, odd.astype(jnp.int32)])
        faces = panel_size // slab

        def mask_of(turn):
            return jnp.where(turn == 0, 1, jnp.where(turn == 1, 3, 0))

        outward, piece2 = pl.pallas_call(
            lambda *refs: outward_kernel(face_dev, *refs),
            grid_spec=pltpu.PrefetchScalarGridSpec(
                num_scalar_prefetch=1,
                grid=(face_dev + faces,),
                in_specs=[
                    pl.BlockSpec(
                        (1, width, width), lambda i, side: (jnp.minimum(i, face_dev - 1), 0, 0)
                    ),
                    pl.BlockSpec(
                        (width, panel_size), lambda i, side: (jnp.minimum(i, face_dev - 1), 0)
                    ),
                    pl.BlockSpec(
                        (slab, face_dev * width),
                        lambda i, side: (
                            jnp.where(
                                side[1] == 1, side[0] ^ FIRST, jnp.maximum(i - face_dev, 0)
                            ),
                            0,
                        ),
                    ),
                ],
                out_specs=[
                    pl.BlockSpec(
                        (width, panel_size), lambda i, side: (jnp.minimum(i, face_dev - 1), 0)
                    ),
                    pl.BlockSpec(
                        (slab, slab), lambda i, side: (0, jnp.maximum(i - face_dev, 0))
                    ),
                ],
                scratch_shapes=[pltpu.VMEM((face_dev * width, panel_size), BF)],
            ),
            out_shape=[
                jax.ShapeDtypeStruct((face_dev * width, panel_size), BF),
                jax.ShapeDtypeStruct((slab, panel_size), BF),
            ],
            compiler_params=pltpu.CompilerParams(vmem_limit_bytes=40 << 20),
            name="outward",
        )(side, inverse_later, coupling_out, coupling_in)
        pieces = pl.pallas_call(
            fold_kernel,
            grid_spec=pltpu.PrefetchScalarGridSpec(
                num_scalar_prefetch=1,
                grid=(x_count - 1, faces),
                in_specs=[
                    pl.BlockSpec(
                        (slab, face_dev * width),
                        lambda i, j, side: (
                            jnp.where(side[1] == 1, side[0] ^ mask_of(i), j),
                            0,
                        ),
                    ),
                    pl.BlockSpec(
                        (face_dev * width, slab),
                        lambda i, j, side: (
                            0,
                            jnp.where(side[1] == 1, j, side[0] ^ mask_of(i)),
                        ),
                    ),
                ],
                out_specs=pl.BlockSpec((1, slab, slab), lambda i, j, side: (i, 0, j)),
            ),
            out_shape=jax.ShapeDtypeStruct((x_count - 1, slab, panel_size), BF),
            compiler_params=pltpu.CompilerParams(vmem_limit_bytes=40 << 20),
            name="fold",
        )(side, coupling_in, outward)
        piece1, piece3, piece0 = pieces[0], pieces[1], pieces[2]
    with jax.named_scope("sum_x"):
        half = slab // 2
        upper = exchange(piece2[:half], 1)
        lower = exchange(piece2[half:], 3)
        to3 = jnp.concatenate([total([piece3[:half], upper]).astype(BF), piece3[half:]], axis=0)
        to1 = jnp.concatenate([piece1[:half], total([piece1[half:], lower]).astype(BF)], axis=0)
        got, to3, to1 = lax.optimization_barrier((got, to3, to1))
        summed_x = total(
            [piece0, exchange(to3, 3), exchange(to1, 1)]
        ).astype(BF)
    with jax.named_scope("source"):
        vmem = pl.BlockSpec(memory_space=pltpu.VMEM)
        assembled, source = pl.pallas_call(
            lambda *refs: source_kernel(face_dev, *refs),
            in_specs=[vmem, vmem, vmem],
            out_specs=[vmem, vmem],
            out_shape=[jax.ShapeDtypeStruct((rhs_count, face_dev * width), F32)] * 2,
            name="source",
        )(got, face_rhs[0], outward)
    with jax.named_scope("sum_source"):
        part = source.astype(BF)
        part = total([part] + [exchange(part, 0, m) for m in range(1, four)]).astype(BF)
        part = total([part, exchange(part, 0, far)]).astype(BF)
        source_parts = [part] + [exchange(part, m) for m in range(1, x_count)]
    with jax.named_scope("sum_z"):
        turns = [z ^ 1 for z in range(z_count)], [3, 6, 5, 0, 7, 2, 1, 4]

        def shifted(places):
            return [(places[(z + 1) % z_count] - 1) % z_count for z in range(z_count)]

        near, across = turns
        paths = [(near, shifted(near), across), (shifted(near), near, shifted(across))]
        part_rows = slab // 2
        bits = [((102 >> z) & 1, (180 >> z) & 1) for z in (here_z, (here_z + 1) % z_count)]
        summed = [summed_x[:part_rows], summed_x[part_rows:]]

        def halved(rows, bit):
            size = rows.shape[0] // 2
            kept = lax.dynamic_slice_in_dim(rows, bit * size, size, 0)
            given = lax.dynamic_slice_in_dim(rows, (1 - bit) * size, size, 0)
            return kept, given

        def joined(own, other, bit):
            size = own.shape[0]
            both = jnp.concatenate([own, own], axis=0)
            return lax.dynamic_update_slice_in_dim(both, other, (1 - bit) * size, 0)

        def swap(values, turn):
            return [exchange(v, 0, 0, along_z=p[turn]) for v, p in zip(values, paths)]

        for turn in range(2):
            split = [halved(rows, bit[turn]) for rows, bit in zip(summed, bits)]
            got_rows = swap([given for _, given in split], turn)
            summed = [total([kept, new]).astype(BF) for (kept, _), new in zip(split, got_rows)]
            if turn == 0:
                source, summed[0] = lax.optimization_barrier((total(source_parts), summed[0]))
        summed = [total([rows, new]).astype(BF) for rows, new in zip(summed, swap(summed, 2))]
        for turn in (1, 0):
            got_rows = swap(summed, turn)
            summed = [
                joined(rows, new, bit[turn]) for rows, new, bit in zip(summed, got_rows, bits)
            ]
        through = jnp.concatenate(summed, axis=0)
        source_slab = lax.dynamic_slice_in_dim(source, here_x * slab, slab, 1)
        source_once = jnp.where(here_x == 0, source, 0.0)
    through_columns = jnp.concatenate(
        [through[:, start : start + slab] for start in range(0, panel_size, slab)], axis=0
    )
    panel = None
    for layer in range(sweep_count - 1):
        with jax.named_scope("stage%d" % layer):
            if layer % 2 == 0:
                following = source_slab
                if panel is not None:
                    following = source_slab - jnp.dot(
                        panel, through_columns, preferred_element_type=F32
                    )
                following = following.astype(BF)
                if layer < sweep_count - 2:
                    panel_slab = exchange(following, 0, 0, after_even)
            else:
                part = source_once - jnp.dot(panel_slab, through, preferred_element_type=F32)
                part = part.astype(BF)
                part = total([exchange(part, m, 0, after_odd) for m in range(x_count)])
                panel = jnp.where(own_layer == 0, 0.0, part).astype(BF)
    with jax.named_scope("spread"):
        spread = jnp.zeros((rhs_count, panel_size), BF)
        for m in range(x_count):
            part = exchange(following, m, 0, after_even)
            spread = lax.dynamic_update_slice_in_dim(spread, part, (here_x ^ m) * slab, 1)
        panel = jnp.where(odd, spread, panel)
    with jax.named_scope("solve"):
        solved = pl.pallas_call(
            solve_kernel,
            in_specs=[vmem] * 4,
            out_specs=vmem,
            out_shape=jax.ShapeDtypeStruct((rhs_count, face_dev, width), F32),
            name="solve",
        )(panel, coupling_in, assembled, inverse)
    return solved[None]


def solution(mesh):
    shape = (mesh.shape["sweep"], 8, mesh.shape["layer"] // 8)
    fine = Mesh(mesh.devices.reshape(shape), ("sweep", "z", "x"))
    layer = ("z", "x")
    everywhere = ("sweep", "z", "x")
    return jax.shard_map(
        lambda *args: on_device(shape, *args),
        mesh=fine,
        in_specs=(
            P("sweep", None, layer, None),
            P(everywhere, None),
            P(everywhere, None),
            P(everywhere),
            P("sweep", layer, None, None),
            P("sweep", None, layer),
            P("sweep", layer, None),
        ),
        out_specs=P("sweep", None, layer, None),
        check_vma=False,
    )
```

```python
import jax
import jax.numpy as jnp
from jax import lax
from jax.experimental import pallas as pl
from jax.experimental.pallas import tpu as pltpu
from jax.sharding import Mesh
from jax.sharding import PartitionSpec as P

BF = jnp.bfloat16
F32 = jnp.float32
LANES = 128
FIRST = 2


def pack_kernel(owner_count, owner_ref, slot_ref, rows_ref, out_ref):
    row_total, width = rows_ref.shape
    capacity = row_total // owner_count * 2
    owner = owner_ref[...]
    match = (lax.broadcasted_iota(jnp.int32, (owner_count, row_total), 0) == owner).astype(F32)
    earlier_mask = (
        lax.broadcasted_iota(jnp.int32, (row_total, row_total), 0)
        < lax.broadcasted_iota(jnp.int32, (row_total, row_total), 1)
    )
    earlier = jnp.dot(
        match.astype(BF), earlier_mask.astype(F32).astype(BF), preferred_element_type=F32
    )
    position = jnp.sum(earlier * match, axis=0, keepdims=True).astype(jnp.int32)
    target = owner * capacity + position
    slots = (slot_ref[...] + 1).astype(F32)
    rows = rows_ref[...].astype(BF)
    block = 256
    for start in range(0, owner_count * capacity, block):
        place = lax.broadcasted_iota(jnp.int32, (block, row_total), 0) + start
        chosen = place == target
        picked = jnp.where(chosen, 1.0, 0.0).astype(BF)
        out_ref[pl.ds(start, block), pl.ds(0, width)] = jnp.dot(
            picked, rows, preferred_element_type=F32
        ).astype(BF)
        slot = jnp.sum(jnp.where(chosen, slots, 0.0), axis=1, keepdims=True)
        out_ref[pl.ds(start, block), pl.ds(width, LANES)] = jnp.broadcast_to(
            slot, (block, LANES)
        ).astype(BF)


def source_kernel(face_dev, got_ref, face_ref, outward_ref, assembled_ref, source_ref):
    rhs_count = assembled_ref.shape[0]
    width = assembled_ref.shape[1] // face_dev
    slot = got_ref[:, pl.ds(width, LANES)].astype(F32)
    lane = lax.broadcasted_iota(jnp.int32, slot.shape, 1)
    wanted = (lane % rhs_count) * face_dev + lane // rhs_count + 1
    wanted = jnp.where(lane < rhs_count * face_dev, wanted, -1).astype(F32)
    picked = jnp.where(slot == wanted, 1.0, 0.0).astype(BF)
    summed = lax.dot_general(
        picked,
        got_ref[:, pl.ds(0, width)],
        (((0,), (0,)), ((), ())),
        preferred_element_type=F32,
    )
    for face in range(face_dev):
        assembled_ref[:, pl.ds(face * width, width)] = (
            face_ref[:, face, :] + summed[face * rhs_count : (face + 1) * rhs_count, :]
        )
    assembled = assembled_ref[...]
    high = assembled.astype(BF)
    low = (assembled - high.astype(F32)).astype(BF)
    both = jnp.dot(
        jnp.concatenate([high, low], axis=0), outward_ref[...], preferred_element_type=F32
    )
    source_ref[...] = both[:rhs_count] + both[rhs_count:]


def outward_kernel(face_dev, side_ref, inv_ref, out_ref, in_ref, outward_ref, piece_ref, held):
    step = pl.program_id(0)
    width = inv_ref.shape[1]

    @pl.when(step < face_dev)
    def _():
        rows = jnp.dot(inv_ref[0], out_ref[...], preferred_element_type=F32).astype(BF)
        outward_ref[...] = rows
        held[pl.ds(pl.multiple_of(step * width, width), width), :] = rows

    @pl.when(step >= face_dev)
    def _():
        block = jnp.where(side_ref[1] == 1, step - face_dev, side_ref[0] ^ FIRST)
        slab = piece_ref.shape[1]
        columns = held[:, pl.ds(pl.multiple_of(block * slab, slab), slab)]
        piece_ref[...] = jnp.dot(in_ref[...], columns, preferred_element_type=F32).astype(BF)


def fold_kernel(side_ref, in_ref, outward_ref, piece_ref):
    piece_ref[0] = jnp.dot(
        in_ref[...], outward_ref[...], preferred_element_type=F32
    ).astype(BF)


def solve_kernel(panel_ref, in_ref, assembled_ref, inv_ref, out_ref):
    coupled = jnp.dot(panel_ref[...], in_ref[...], preferred_element_type=F32)
    local = (assembled_ref[...] - coupled).astype(BF)
    width = inv_ref.shape[1]
    for face in range(inv_ref.shape[0]):
        out_ref[:, face, :] = jnp.dot(
            local[:, face * width : (face + 1) * width], inv_ref[face], preferred_element_type=F32
        )


def on_device(shape, face_rhs, res_rows, row_owner, row_slot, inv_blocks, couple_in, couple_out):
    sweep_count, z_count, x_count = shape
    group_size = z_count * x_count
    rhs_count, face_dev, width = face_rhs.shape[1:]
    row_total = res_rows.shape[0]
    capacity = 2 * row_total // group_size
    coupling_in, coupling_out, inverse = couple_in[0], couple_out[0], inv_blocks[0]

    def number(s, z, x):
        return (s * z_count + z) * x_count + x

    def exchange(value, mask_x, mask_z=0, partner=lambda s: s, along_z=None):
        pairs = [
            (
                number(s, z, x),
                number(partner(s), along_z[z] if along_z else z ^ mask_z, x ^ mask_x),
            )
            for s in range(sweep_count)
            for z in range(z_count)
            for x in range(x_count)
        ]
        return lax.ppermute(value, ("sweep", "z", "x"), pairs)

    def after_even(s):
        return s ^ 1

    def after_odd(s):
        return (s + 1 if s % 2 else s - 1) % sweep_count

    def total(values):
        result = values[0].astype(F32)
        for value in values[1:]:
            result = result + value.astype(F32)
        return result

    far, four = z_count - 1, z_count // 2
    here_x, here_z = lax.axis_index("x"), lax.axis_index("z")
    own_layer = lax.axis_index("sweep")
    odd = own_layer % 2 == 1
    panel_size = coupling_in.shape[0]
    slab = panel_size // x_count

    with jax.named_scope("pack"):
        packed = pl.pallas_call(
            lambda *refs: pack_kernel(group_size, *refs),
            out_shape=jax.ShapeDtypeStruct((group_size * capacity, width + LANES), BF),
            name="pack",
        )(row_owner.reshape(1, row_total), row_slot.reshape(1, row_total), res_rows)
    with jax.named_scope("route"):
        inverse_later, packed = lax.optimization_barrier((inverse, packed))
        got = lax.all_to_all(
            packed.reshape(group_size, capacity, width + LANES),
            ("z", "x"),
            split_axis=0,
            concat_axis=0,
            tiled=True,
        ).reshape(group_size * capacity, width + LANES)
    with jax.named_scope("fold"):
        side = jnp.stack([here_x, odd.astype(jnp.int32)])
        faces = panel_size // slab

        def mask_of(turn):
            return jnp.where(turn == 0, 1, jnp.where(turn == 1, 3, 0))

        outward, piece2 = pl.pallas_call(
            lambda *refs: outward_kernel(face_dev, *refs),
            grid_spec=pltpu.PrefetchScalarGridSpec(
                num_scalar_prefetch=1,
                grid=(face_dev + faces,),
                in_specs=[
                    pl.BlockSpec(
                        (1, width, width), lambda i, side: (jnp.minimum(i, face_dev - 1), 0, 0)
                    ),
                    pl.BlockSpec(
                        (width, panel_size), lambda i, side: (jnp.minimum(i, face_dev - 1), 0)
                    ),
                    pl.BlockSpec(
                        (slab, face_dev * width),
                        lambda i, side: (
                            jnp.where(
                                side[1] == 1, side[0] ^ FIRST, jnp.maximum(i - face_dev, 0)
                            ),
                            0,
                        ),
                    ),
                ],
                out_specs=[
                    pl.BlockSpec(
                        (width, panel_size), lambda i, side: (jnp.minimum(i, face_dev - 1), 0)
                    ),
                    pl.BlockSpec(
                        (slab, slab), lambda i, side: (0, jnp.maximum(i - face_dev, 0))
                    ),
                ],
                scratch_shapes=[pltpu.VMEM((face_dev * width, panel_size), BF)],
            ),
            out_shape=[
                jax.ShapeDtypeStruct((face_dev * width, panel_size), BF),
                jax.ShapeDtypeStruct((slab, panel_size), BF),
            ],
            compiler_params=pltpu.CompilerParams(vmem_limit_bytes=40 << 20),
            name="outward",
        )(side, inverse_later, coupling_out, coupling_in)
        pieces = pl.pallas_call(
            fold_kernel,
            grid_spec=pltpu.PrefetchScalarGridSpec(
                num_scalar_prefetch=1,
                grid=(x_count - 1, faces),
                in_specs=[
                    pl.BlockSpec(
                        (slab, face_dev * width),
                        lambda i, j, side: (
                            jnp.where(side[1] == 1, side[0] ^ mask_of(i), j),
                            0,
                        ),
                    ),
                    pl.BlockSpec(
                        (face_dev * width, slab),
                        lambda i, j, side: (
                            0,
                            jnp.where(side[1] == 1, j, side[0] ^ mask_of(i)),
                        ),
                    ),
                ],
                out_specs=pl.BlockSpec((1, slab, slab), lambda i, j, side: (i, 0, j)),
            ),
            out_shape=jax.ShapeDtypeStruct((x_count - 1, slab, panel_size), BF),
            compiler_params=pltpu.CompilerParams(vmem_limit_bytes=40 << 20),
            name="fold",
        )(side, coupling_in, outward)
        piece1, piece3, piece0 = pieces[0], pieces[1], pieces[2]
    with jax.named_scope("sum_x"):
        half = slab // 2
        upper = exchange(piece2[:half], 1)
        lower = exchange(piece2[half:], 3)
        to3 = jnp.concatenate([total([piece3[:half], upper]).astype(BF), piece3[half:]], axis=0)
        to1 = jnp.concatenate([piece1[:half], total([piece1[half:], lower]).astype(BF)], axis=0)
        got, to3, to1 = lax.optimization_barrier((got, to3, to1))
        summed_x = total(
            [piece0, exchange(to3, 3), exchange(to1, 1)]
        ).astype(BF)
    with jax.named_scope("source"):
        vmem = pl.BlockSpec(memory_space=pltpu.VMEM)
        assembled, source = pl.pallas_call(
            lambda *refs: source_kernel(face_dev, *refs),
            in_specs=[vmem, vmem, vmem],
            out_specs=[vmem, vmem],
            out_shape=[jax.ShapeDtypeStruct((rhs_count, face_dev * width), F32)] * 2,
            name="source",
        )(got, face_rhs[0], outward)
    with jax.named_scope("sum_source"):
        part = source.astype(BF)
        part = total([part] + [exchange(part, 0, m) for m in range(1, four)]).astype(BF)
        part = total([part, exchange(part, 0, far)]).astype(BF)
        source_parts = [part] + [exchange(part, m) for m in range(1, x_count)]
    with jax.named_scope("sum_z"):
        turns = [z ^ 1 for z in range(z_count)], [3, 6, 5, 0, 7, 2, 1, 4]

        def shifted(places):
            return [(places[(z + 1) % z_count] - 1) % z_count for z in range(z_count)]

        near, across = turns
        paths = [(near, shifted(near), across), (shifted(near), near, shifted(across))]
        part_rows = slab // 2
        bits = [((102 >> z) & 1, (180 >> z) & 1) for z in (here_z, (here_z + 1) % z_count)]
        summed = [summed_x[:part_rows], summed_x[part_rows:]]

        def halved(rows, bit):
            size = rows.shape[0] // 2
            kept = lax.dynamic_slice_in_dim(rows, bit * size, size, 0)
            given = lax.dynamic_slice_in_dim(rows, (1 - bit) * size, size, 0)
            return kept, given

        def joined(own, other, bit):
            size = own.shape[0]
            both = jnp.concatenate([own, own], axis=0)
            return lax.dynamic_update_slice_in_dim(both, other, (1 - bit) * size, 0)

        def swap(values, turn):
            return [exchange(v, 0, 0, along_z=p[turn]) for v, p in zip(values, paths)]

        for turn in range(2):
            split = [halved(rows, bit[turn]) for rows, bit in zip(summed, bits)]
            got_rows = swap([given for _, given in split], turn)
            summed = [total([kept, new]).astype(BF) for (kept, _), new in zip(split, got_rows)]
            if turn == 0:
                source, summed[0] = lax.optimization_barrier((total(source_parts), summed[0]))
        summed = [total([rows, new]).astype(BF) for rows, new in zip(summed, swap(summed, 2))]
        for turn in (1, 0):
            got_rows = swap(summed, turn)
            summed = [
                joined(rows, new, bit[turn]) for rows, new, bit in zip(summed, got_rows, bits)
            ]
        through = jnp.concatenate(summed, axis=0)
        source_slab = lax.dynamic_slice_in_dim(source, here_x * slab, slab, 1)
        source_once = jnp.where(here_x == 0, source, 0.0)
    through_columns = jnp.concatenate(
        [through[:, start : start + slab] for start in range(0, panel_size, slab)], axis=0
    )
    panel = None
    for layer in range(sweep_count - 1):
        with jax.named_scope("stage%d" % layer):
            if layer % 2 == 0:
                following = source_slab
                if panel is not None:
                    following = source_slab - jnp.dot(
                        panel, through_columns, preferred_element_type=F32
                    )
                following = following.astype(BF)
                if layer < sweep_count - 2:
                    panel_slab = exchange(following, 0, 0, after_even)
            else:
                part = source_once - jnp.dot(panel_slab, through, preferred_element_type=F32)
                part = part.astype(BF)
                part = total([exchange(part, m, 0, after_odd) for m in reversed(range(x_count))])
                panel = jnp.where(own_layer == 0, 0.0, part).astype(BF)
    with jax.named_scope("spread"):
        spread = jnp.zeros((rhs_count, panel_size), BF)
        for m in range(x_count):
            part = exchange(following, m, 0, after_even)
            spread = lax.dynamic_update_slice_in_dim(spread, part, (here_x ^ m) * slab, 1)
        panel = jnp.where(odd, spread, panel)
    with jax.named_scope("solve"):
        solved = pl.pallas_call(
            solve_kernel,
            in_specs=[vmem] * 4,
            out_specs=vmem,
            out_shape=jax.ShapeDtypeStruct((rhs_count, face_dev, width), F32),
            name="solve",
        )(panel, coupling_in, assembled, inverse)
    return solved[None]


def solution(mesh):
    shape = (mesh.shape["sweep"], 8, mesh.shape["layer"] // 8)
    fine = Mesh(mesh.devices.reshape(shape), ("sweep", "z", "x"))
    layer = ("z", "x")
    everywhere = ("sweep", "z", "x")
    return jax.shard_map(
        lambda *args: on_device(shape, *args),
        mesh=fine,
        in_specs=(
            P("sweep", None, layer, None),
            P(everywhere, None),
            P(everywhere, None),
            P(everywhere),
            P("sweep", layer, None, None),
            P("sweep", None, layer),
            P("sweep", layer, None),
        ),
        out_specs=P("sweep", None, layer, None),
        check_vma=False,
    )
```
